512 devices in a mesh: row: 16 (over z_hi, x, core), col: 8 (over z_lo), blk: 4 (over y).
Axes of the slice: x: 4, y: 4, z: 16 (z_hi: 2, z_lo: 8; z = z_hi * 8 + z_lo), core: 2. Of those that a mesh axis runs over, the one named last changes fastest.
Arguments:
- amplitudes: float32 [32, 32, 256, 256], P('row', None, ('col', 'blk')), may hold values from -6 to 6
- ladder_ints: float32 [32, 256, 256, 256], P('row', None, ('col', 'blk')), may hold values from -0.0234375 to 0.0234375
- cycle_direct: float32 [32, 32, 32, 256], P(None, 'row', None, ('col', 'blk')), may hold values from -0.0625 to 0.0625
- cycle_cross: float32 [32, 32, 32, 256], P(None, 'row', None, ('col', 'blk')), may hold values from -0.0625 to 0.0625
- eps_occ: float32 [32], replicated, may hold values from -1 to -0.25
- eps_vir: float32 [256], replicated, may hold values from 0.25 to 1.5
Outputs:
- update: float32 [32, 32, 32, 256], P(('col', 'blk'), None, 'row')
The draws below stay inside these ranges and needn't reach their ends.
All inputs are finite; a program needn't handle non-finite values.
Results may differ from the reference program's by a relative error of at most 0.00007.
Values sent between devices are 32-bit elements; how exact they have to be, the bound alone decides.
No kernel may reach another device: no remote copies, remote signals or barrier semaphores. Data moves between devices by JAX's collectives and lax.ppermute only.
A program may use at most 128 MiB of HBM per device.

```python
import jax
import jax.numpy as jnp
from jax import lax

O = 32
V = 256
SLAB = 32


def block_levels(key, shape, split, least, high):
    factor_of, own = 1.0, jax.random.fold_in(key, 6)
    for position, parts in split:
        steps = jnp.exp(jax.random.uniform(jax.random.fold_in(own, position), (parts,), jnp.float32, least / len(split), high / len(split)))
        factor_of = factor_of * jnp.repeat(steps, shape[position] // parts).reshape([-1 if axis == position else 1 for axis in range(len(shape))])
    return factor_of


def normal_values(rng, extent, width, most, split=(), held_as=jnp.bfloat16):
    drawn = width * jax.random.normal(rng, extent, jnp.float32)
    if split:
        drawn = drawn * block_levels(rng, extent, split, -0.22, 0.18)
    return jnp.clip(drawn, -most, most).astype(held_as)


def setup_inputs(seed: int = 0) -> dict:
    splits = jax.random.split(jax.random.key(seed), 7)
    return {
        "amplitudes": normal_values(splits[0], (O, O, V, V), 1.0, 6.0, ((0, 16), (2, 32)), jnp.float32),
        "ladder_ints": normal_values(splits[1], (SLAB, V, V, V), (V * V) ** -0.5, 0.0234375, ((0, 16), (2, 32)), jnp.float32),
        "cycle_direct": normal_values(splits[2], (O, SLAB, O, V), (O * V) ** -0.5, 0.0625, ((1, 16), (3, 32)), jnp.float32),
        "cycle_cross": normal_values(splits[3], (O, SLAB, O, V), (O * V) ** -0.5, 0.0625, ((1, 16), (3, 32)), jnp.float32),
        "eps_occ": jnp.clip(jax.random.uniform(splits[4], (O,), jnp.float32, -1.0, -0.25), -1.0, -0.25),
        "eps_vir": jnp.clip(jax.random.uniform(splits[5], (V,), jnp.float32, 0.25, 1.5), 0.25, 1.5),
    }


def reference(amplitudes, ladder_ints, cycle_direct, cycle_cross, eps_occ, eps_vir):
    precise = lax.Precision.HIGHEST
    ladder_term = lax.dot_general(amplitudes.reshape(O * O, V * V), ladder_ints.reshape(SLAB * V, V * V), (((1,), (1,)), ((), ())), precision=precise, preferred_element_type=jnp.float32).reshape(O, O, SLAB, V)
    direct_term = jnp.einsum('iakc,kjcb->ijab', cycle_direct, amplitudes, precision=precise)
    cross_term = jnp.einsum('iakc,kjbc->ijab', cycle_cross, amplitudes, precision=precise)
    residual_sum = ladder_term + direct_term - cross_term
    slab_energy = eps_vir[:SLAB]
    denominator = eps_occ[:, None, None, None] + eps_occ[None, :, None, None] - slab_energy[None, None, :, None] - eps_vir[None, None, None, :]
    return residual_sum / denominator
```

```python
import jax
import jax.numpy as jnp
from jax import lax
from jax.experimental import pallas as pl
from jax.experimental.pallas import tpu as pltpu
from jax.sharding import Mesh, PartitionSpec as P

CHUNKS = 2
VMEM = pl.BlockSpec(memory_space=pltpu.VMEM)
SMEM = pl.BlockSpec(memory_space=pltpu.SMEM)


def halves(value):
    high = value.astype(jnp.bfloat16)
    return high, (value - high.astype(jnp.float32)).astype(jnp.bfloat16)


def mul(a, b):
    return lax.dot_general(a, b, (((1,), (0,)), ((), ())), preferred_element_type=jnp.float32)


def every_eighth(lanes, first, count):
    return jnp.concatenate([lanes[n, pl.ds(first, count, stride=8), :] for n in range(2)], axis=1)


def swap(value, axis, bit):
    length = lax.axis_size(axis)
    return lax.ppermute(value, axis, [(i, i ^ bit) for i in range(length)])


def across(value):
    pairs = [(2 * z + c, 2 * (1 - z) + (1 - c)) for z in range(2) for c in range(2)]
    return lax.ppermute(value, ("zh", "core"), pairs)


def weights_kernel(w_ref, high_ref, low_ref, lanes):
    rows = high_ref.shape[1]
    lanes[0] = w_ref[:, :128]
    lanes[1] = w_ref[:, 128:]
    for c in range(8):
        block = every_eighth(lanes, c, rows)
        high, low = halves(block.T)
        high_ref[pl.ds(c * 256, 256), :] = high
        low_ref[pl.ds(c * 256, 256), :] = low


def weights(integrals):
    flat = integrals.reshape(-1, 256)
    rows = flat.shape[0] // 8
    step = 128
    return pl.pallas_call(
        weights_kernel,
        grid=(rows // step,),
        in_specs=[pl.BlockSpec((step * 8, 256), lambda n: (n, 0))],
        out_specs=[pl.BlockSpec((2048, step), lambda n: (0, n))] * 2,
        out_shape=[jax.ShapeDtypeStruct((2048, rows), jnp.bfloat16)] * 2,
        scratch_shapes=[pltpu.VMEM((2, step * 8, 128), jnp.float32)],
        cost_estimate=pl.CostEstimate(flops=0, bytes_accessed=32 << 20, transcendentals=0),
    )(flat)


def cross_kernel(place, own_ref, other_ref, high_ref, low_ref, rows_ref):
    core, position = place[0], place[1]
    for which, ref in ((core, own_ref), (1 - core, other_ref)):

        def one(k, carry, which=which, ref=ref):
            for near in range(4):
                for far in range(8):
                    bits = ((far >> 2) & 1) | (far & 2) | ((far & 1) << 2)
                    target = (bits * 4 + near) ^ position
                    rows_ref[pl.ds(pl.multiple_of(target * 8, 8), 8), :] = ref[near, far, k]
            high, low = halves(rows_ref[...])
            high_ref[which, k] = high
            low_ref[which, k] = low
            return carry

        lax.fori_loop(0, own_ref.shape[2], one, 0)


def cross_weights(place, own, other):
    shape = (2, own.shape[2], 256, 128)
    return pl.pallas_call(
        cross_kernel,
        in_specs=[SMEM, VMEM, VMEM],
        out_specs=[VMEM] * 2,
        out_shape=[jax.ShapeDtypeStruct(shape, jnp.bfloat16)] * 2,
        scratch_shapes=[pltpu.VMEM((256, 128), jnp.float32)],
        cost_estimate=pl.CostEstimate(flops=0, bytes_accessed=16 << 20, transcendentals=0),
    )(place, own, other)


def terms_kernel(place, *refs):
    t = refs[:8]
    w_high, w_low, v_high, v_low, x_ref, y_high, y_low = refs[8:15]
    outs = refs[15:19]
    acc, lanes = refs[19:]
    core, position, near, target = place[0], place[1], place[2], place[3]
    span = t[0].shape[0] // 4
    js = span // 8

    for n, ref in enumerate(t):
        for half in range(2):
            lanes[half, pl.ds(n * 4 * span, 4 * span), :] = ref[:, half * 128 : half * 128 + 128]

    for c in range(8):
        high, low = halves(every_eighth(lanes, c, 32 * js))
        for which, wh, wl in ((core, w_high, w_low), (1 - core, v_high, v_low)):
            part = (
                mul(high, wh[pl.ds(c * 256, 256), :])
                + mul(low, wh[pl.ds(c * 256, 256), :])
                + mul(high, wl[pl.ds(c * 256, 256), :])
            )
            for n in range(4):
                piece = part[:, n * 128 : n * 128 + 128]
                if c == 0:
                    acc[which * 4 + n] = piece
                else:
                    acc[which * 4 + n] += piece

    cross = jnp.zeros((span, 128), jnp.float32)
    for q in range(8):
        for s in range(4):
            high, low = halves(t[q][pl.ds(s * span, span), :])
            wh, wl = y_high[s // 2, q * 2 + s % 2], y_low[s // 2, q * 2 + s % 2]
            cross += mul(high, wh) + mul(low, wh) + mul(high, wl)
    lane = lax.broadcasted_iota(jnp.int32, (8, 256), 1)
    line = lax.broadcasted_iota(jnp.int32, (8, 256), 0)
    spread = jnp.where(lane == position * 8 + line, -1.0, 0.0).astype(jnp.bfloat16)
    x_high, x_low = halves(x_ref[...])
    turned = cross.T
    for j in range(js):
        rows = jnp.concatenate(
            [t[q][pl.ds((s * js + j) * 8, 8), :] for q in range(8) for s in range(4)], axis=0
        )
        high, low = halves(rows)
        c_high, c_low = halves(turned[:, j * 8 : j * 8 + 8])
        part = (
            mul(x_high, high)
            + mul(x_low, high)
            + mul(x_high, low)
            + mul(c_high, spread)
            + mul(c_low, spread)
        )
        for n in range(8):
            where = (n, pl.ds(j, 32, stride=js), slice(None))
            a, half = n // 2, n % 2
            acc[where] += part[a * 32 : a * 32 + 32, half * 128 : half * 128 + 128]

    for d in range(4):
        for v in range(8):
            bits = ((v >> 2) & 1) | (v & 2) | ((v & 1) << 2)
            row = ((bits ^ target) * 4 + (near ^ d)) * js
            for n in range(8):
                outs[d][v, :, n * 128 : n * 128 + 128] = acc[
                    n, pl.ds(pl.multiple_of(row, 8), js), :
                ]


def terms(place, pieces, w, v, x, y):
    js = pieces[0].shape[0] // 32
    rows = 32 * js
    return pl.pallas_call(
        terms_kernel,
        in_specs=[SMEM] + [VMEM] * 15,
        out_specs=[VMEM] * 4,
        out_shape=[jax.ShapeDtypeStruct((8, js, 1024), jnp.float32)] * 4,
        scratch_shapes=[
            pltpu.VMEM((8, rows, 128), jnp.float32),
            pltpu.VMEM((2, rows * 8, 128), jnp.float32),
        ],
        cost_estimate=pl.CostEstimate(
            flops=6 * rows * 1024 * 2048 * 3, bytes_accessed=16 << 20, transcendentals=0
        ),
    )(place, *pieces, *w, *v, x, *y)


def both(core, own, other, dim=0):
    return jnp.where(
        core == 0, jnp.concatenate([own, other], dim), jnp.concatenate([other, own], dim)
    )


def turn(value, dim, flips):
    return jnp.take(value, jnp.arange(8) ^ flips, axis=dim, unique_indices=True, mode="clip")


def body(amplitudes, ladder_ints, cycle_direct, cycle_cross, eps_occ, eps_vir):
    zh, x, core = lax.axis_index("zh"), lax.axis_index("x"), lax.axis_index("core")
    zl, y = lax.axis_index("zl"), lax.axis_index("y")
    group = zh * 4 + x
    place = jnp.stack([core, zl * 4 + y, y, zl ^ group]).astype(jnp.int32)

    parts = amplitudes.reshape(2, 2, CHUNKS, -1, 8, 256)
    mine = lax.dynamic_index_in_dim(parts, core, 1, keepdims=False)
    theirs = lax.dynamic_index_in_dim(parts, 1 - core, 1, keepdims=False)
    far = [
        (swap(mine[:, n], "zh", 1), across(theirs[:, n])) for n in range(CHUNKS)
    ]
    got = swap(theirs, "core", 1)
    held = both(core, mine, got)
    near = [held[:, n] for n in range(CHUNKS)]
    beside = [[swap(near[n], "x", s) for s in (1, 3, 2)] for n in range(CHUNKS)]

    def ordered(value):
        value = turn(turn(value.reshape(8, 4, 2, 8, 4, 8), 0, group), 3, group)
        return value.transpose(3, 4, 5, 2, 0, 1).reshape(32, 8, 64)

    local = jnp.stack([ordered(cycle_direct), ordered(cycle_cross)])
    paired = both(core, local, swap(local, "core", 1), 3)
    x_rows = paired[0].reshape(256, 128).T
    y_local = lax.dynamic_index_in_dim(
        paired[1].reshape(8, 2, 2, 8, 128), core, 1, keepdims=False
    ).reshape(16, 8, 128)
    for bit in (4, 2, 1):
        y_local = jnp.stack([y_local, swap(y_local, "zl", bit)])
    y_local = y_local.reshape(8, 16, 8, 128)
    ys = jnp.stack([y_local] + [swap(y_local, "y", s) for s in (1, 2, 3)])
    y = cross_weights(place, ys, swap(ys, "core", 1))

    w = weights(ladder_ints)
    v = weights(swap(ladder_ints, "core", 1))

    done = []
    for n in range(CHUNKS):
        arrived = both(core, *far[n])
        away = [swap(arrived, "x", s) for s in (1, 3, 2)]
        pieces = [near[n], beside[n][0], beside[n][2], beside[n][1]]
        pieces += [arrived, away[0], away[2], away[1]]
        pieces = [piece.reshape(-1, 256) for piece in pieces]
        outs = terms(place, pieces, w, v, x_rows, y)
        total = outs[0] + (
            swap(outs[1], "y", 1) + swap(outs[3], "y", 3) + swap(outs[2], "y", 2)
        )
        for bit in (1, 2, 4):
            half = total.shape[0] // 2
            total = total[:half] + swap(total[half:], "zl", bit)
        done.append(total[0])
    total = jnp.concatenate(done, 0).reshape(-1, 2, 512)
    kept = lax.dynamic_index_in_dim(total, core, 1, keepdims=False)
    sent = lax.dynamic_index_in_dim(total, 1 - core, 1, keepdims=False)
    residual = both(core, kept, swap(sent, "core", 1)).reshape(1, 32, 2, 256)

    row = group * 2 + core
    occ_energy = lax.dynamic_slice_in_dim(eps_occ, zl * 4 + lax.axis_index("y"), 1, 0)
    slab_energy = lax.dynamic_slice_in_dim(eps_vir, row * 2, 2, 0)
    denominator = (
        occ_energy[:, None, None, None]
        + eps_occ[None, :, None, None]
        - slab_energy[None, None, :, None]
        - eps_vir[None, None, None, :]
    )
    return residual / denominator


def solution(mesh):
    split = Mesh(mesh.devices.reshape(2, 4, 2, 8, 4), ("zh", "x", "core", "zl", "y"))
    row, inner = ("zh", "x", "core"), ("zl", "y")
    return jax.shard_map(
        body,
        mesh=split,
        in_specs=(
            P(row, None, inner, None),
            P(row, None, inner, None),
            P(None, row, None, inner),
            P(None, row, None, inner),
            P(),
            P(),
        ),
        out_specs=P(inner, None, row, None),
        check_vma=False,
    )
```

```python
import functools

import jax
import jax.numpy as jnp
from jax import lax
from jax.experimental import pallas as pl
from jax.experimental.pallas import tpu as pltpu
from jax.sharding import Mesh, PartitionSpec as P


VMEM = pl.BlockSpec(memory_space=pltpu.VMEM)
SMEM = pl.BlockSpec(memory_space=pltpu.SMEM)


def halves(value):
    high = value.astype(jnp.bfloat16)
    return high, (value - high.astype(jnp.float32)).astype(jnp.bfloat16)


def mul(a, b):
    return lax.dot_general(a, b, (((1,), (0,)), ((), ())), preferred_element_type=jnp.float32)


def every_eighth(lanes, first, count):
    return jnp.concatenate([lanes[n, pl.ds(first, count, stride=8), :] for n in range(2)], axis=1)


def swap(value, axis, bit):
    length = lax.axis_size(axis)
    return lax.ppermute(value, axis, [(i, i ^ bit) for i in range(length)])


def weights_kernel(w_ref, high_ref, low_ref, lanes):
    rows = high_ref.shape[1]
    lanes[0] = w_ref[:, :128]
    lanes[1] = w_ref[:, 128:]
    for c in range(8):
        block = every_eighth(lanes, c, rows)
        high, low = halves(block.T)
        high_ref[pl.ds(c * 256, 256), :] = high
        low_ref[pl.ds(c * 256, 256), :] = low


def weights(integrals):
    flat = integrals.reshape(-1, 256)
    rows = flat.shape[0] // 8
    step = 128
    return pl.pallas_call(
        weights_kernel,
        grid=(rows // step,),
        in_specs=[pl.BlockSpec((step * 8, 256), lambda n: (n, 0))],
        out_specs=[pl.BlockSpec((2048, step), lambda n: (0, n))] * 2,
        out_shape=[jax.ShapeDtypeStruct((2048, rows), jnp.bfloat16)] * 2,
        scratch_shapes=[pltpu.VMEM((2, step * 8, 128), jnp.float32)],
        cost_estimate=pl.CostEstimate(flops=0, bytes_accessed=32 << 20, transcendentals=0),
    )(flat)


def cross_kernel(place, own_ref, other_ref, high_ref, low_ref, rows_ref):
    core, position = place[0], place[1]
    for which, ref in ((core, own_ref), (1 - core, other_ref)):

        def one(k, carry, which=which, ref=ref):
            for near in range(4):
                for far in range(8):
                    bits = ((far >> 2) & 1) | (far & 2) | ((far & 1) << 2)
                    target = (bits * 4 + near) ^ position
                    rows_ref[pl.ds(pl.multiple_of(target * 8, 8), 8), :] = ref[near, far, k]
            high, low = halves(rows_ref[...])
            high_ref[which, k] = high
            low_ref[which, k] = low
            return carry

        lax.fori_loop(0, own_ref.shape[2], one, 0)


def cross_weights(place, own, other):
    shape = (2, own.shape[2], 256, 128)
    return pl.pallas_call(
        cross_kernel,
        in_specs=[SMEM, VMEM, VMEM],
        out_specs=[VMEM] * 2,
        out_shape=[jax.ShapeDtypeStruct(shape, jnp.bfloat16)] * 2,
        scratch_shapes=[pltpu.VMEM((256, 128), jnp.float32)],
        cost_estimate=pl.CostEstimate(flops=0, bytes_accessed=16 << 20, transcendentals=0),
    )(place, own, other)


def terms_kernel(place, *refs, late):
    t = refs[: 8 if late else 4]
    refs = refs[len(t) :]
    w_high, w_low, v_high, v_low, x_ref = refs[:5]
    if late:
        y_high, y_low, start = refs[5:8]
        outs, (acc, lanes) = refs[8:12], refs[12:]
    else:
        acc, lanes = refs[5:]
    core, position, near, target = place[0], place[1], place[2], place[3]
    span = t[0].shape[0] // 4
    js = span // 8
    now = t[4:] if late else t
    first = 16 * js if late else 0
    if late:
        acc[...] = start[...]
    else:
        acc[:, pl.ds(16 * js, 16 * js), :] = jnp.zeros((8, 16 * js, 128), jnp.float32)
    for n, ref in enumerate(now):
        for half in range(2):
            lanes[half, pl.ds(n * 4 * span, 4 * span), :] = ref[:, half * 128 : half * 128 + 128]

    for c in range(8):
        high, low = halves(every_eighth(lanes, c, 16 * js))
        for which, wh, wl in ((core, w_high, w_low), (1 - core, v_high, v_low)):
            part = (
                mul(high, wh[pl.ds(c * 256, 256), :])
                + mul(low, wh[pl.ds(c * 256, 256), :])
                + mul(high, wl[pl.ds(c * 256, 256), :])
            )
            for n in range(4):
                piece = part[:, n * 128 : n * 128 + 128]
                if c == 0 and not late:
                    acc[which * 4 + n, pl.ds(first, 16 * js), :] = piece
                else:
                    acc[which * 4 + n, pl.ds(first, 16 * js), :] += piece

    if late:
        cross = jnp.zeros((span, 128), jnp.float32)
        for q in range(8):
            for s in range(4):
                high, low = halves(t[q][pl.ds(s * span, span), :])
                wh, wl = y_high[s // 2, q * 2 + s % 2], y_low[s // 2, q * 2 + s % 2]
                cross += mul(high, wh) + mul(low, wh) + mul(high, wl)
        lane = lax.broadcasted_iota(jnp.int32, (8, 256), 1)
        line = lax.broadcasted_iota(jnp.int32, (8, 256), 0)
        spread = jnp.where(lane == position * 8 + line, -1.0, 0.0).astype(jnp.bfloat16)
        turned = cross.T
    x_high, x_low = halves(x_ref[:, 128:] if late else x_ref[:, :128])
    for j in range(js):
        rows = jnp.concatenate(
            [ref[pl.ds((s * js + j) * 8, 8), :] for ref in now for s in range(4)], axis=0
        )
        high, low = halves(rows)
        part = mul(x_high, high) + mul(x_low, high) + mul(x_high, low)
        if late:
            c_high, c_low = halves(turned[:, j * 8 : j * 8 + 8])
            part += mul(c_high, spread) + mul(c_low, spread)
        for n in range(8):
            where = (n, pl.ds(j, 32, stride=js), slice(None))
            a, half = n // 2, n % 2
            acc[where] += part[a * 32 : a * 32 + 32, half * 128 : half * 128 + 128]

    if late:
        for d in range(4):
            for v in range(8):
                bits = ((v >> 2) & 1) | (v & 2) | ((v & 1) << 2)
                row = ((bits ^ target) * 4 + (near ^ d)) * js
                for n in range(8):
                    outs[d][v, :, n * 128 : n * 128 + 128] = acc[
                        n, pl.ds(pl.multiple_of(row, 8), js), :
                    ]


def terms(place, pieces, w, v, x, y=(), start=None):
    late = start is not None
    js = pieces[0].shape[0] // 32
    rows = 32 * js
    whole = jax.ShapeDtypeStruct((8, rows, 128), jnp.float32)
    args = (*pieces, *w, *v, x, *y) + ((start,) if late else ())
    lanes = pltpu.VMEM((2, rows * 4, 128), jnp.float32)
    return pl.pallas_call(
        functools.partial(terms_kernel, late=late),
        in_specs=[SMEM] + [VMEM] * len(args),
        out_specs=[VMEM] * 4 if late else VMEM,
        out_shape=[jax.ShapeDtypeStruct((8, js, 1024), jnp.float32)] * 4 if late else whole,
        scratch_shapes=[pltpu.VMEM(whole.shape, jnp.float32), lanes] if late else [lanes],
        cost_estimate=pl.CostEstimate(
            flops=3 * rows * 1024 * 2048, bytes_accessed=20 << 20, transcendentals=0
        ),
    )(place, *args)


def both(core, own, other, dim=0):
    return jnp.where(
        core == 0, jnp.concatenate([own, other], dim), jnp.concatenate([other, own], dim)
    )


def turn(value, dim, flips):
    return jnp.take(value, jnp.arange(8) ^ flips, axis=dim, unique_indices=True, mode="clip")


def step(amplitudes, ladder_ints, cycle_direct, cycle_cross, eps_occ, eps_vir):
    zh, x, core = lax.axis_index("zh"), lax.axis_index("x"), lax.axis_index("core")
    zl, y = lax.axis_index("zl"), lax.axis_index("y")
    group = zh * 4 + x
    place = jnp.stack([core, zl * 4 + y, y, zl ^ group]).astype(jnp.int32)

    parts = amplitudes.reshape(2, 2, -1, 8, 256)
    mine = lax.dynamic_index_in_dim(parts, core, 1, keepdims=False)
    theirs = lax.dynamic_index_in_dim(parts, 1 - core, 1, keepdims=False)
    held = both(core, mine, swap(theirs, "core", 1))
    arrived = swap(held, "zh", 1)
    cycle_direct, cycle_cross, held = lax.optimization_barrier((cycle_direct, cycle_cross, held))
    pieces = [held] + [swap(held, "x", s) for s in (1, 2, 3)]

    def ordered(value):
        value = turn(turn(value.reshape(8, 4, 2, 8, 4, 8), 0, group), 3, group)
        return value.transpose(3, 4, 5, 2, 0, 1).reshape(32, 8, 64)

    local = jnp.stack([ordered(cycle_direct), ordered(cycle_cross)])
    paired = both(core, local, swap(local, "core", 1), 3)
    x_rows = paired[0].reshape(256, 128).T
    y_local = lax.dynamic_index_in_dim(
        paired[1].reshape(8, 2, 2, 8, 128), core, 1, keepdims=False
    ).reshape(16, 8, 128)
    for bit in (4, 2, 1):
        y_local = jnp.stack([y_local, swap(y_local, "zl", bit)])
    y_local = y_local.reshape(8, 16, 8, 128)
    ys = jnp.stack([y_local] + [swap(y_local, "y", s) for s in (1, 2, 3)])
    cross = cross_weights(place, ys, swap(ys, "core", 1))

    swapped = swap(ladder_ints, "core", 1)
    w = weights(ladder_ints)
    v = weights(swapped)

    def flat(values):
        return [value.reshape(-1, 256) for value in values]

    start = terms(place, flat(pieces), w, v, x_rows)
    pieces += [arrived] + [swap(arrived, "x", s) for s in (1, 2, 3)]
    outs = terms(place, flat(pieces), w, v, x_rows, cross, start)
    moved = {d: swap(outs[d], "y", d) for d in (2, 1, 3)}
    total = outs[0] + moved[1] + moved[3] + moved[2]
    for bit in (1, 2, 4):
        half = total.shape[0] // 2
        total = total[:half] + swap(total[half:], "zl", bit)
    total = total[0].reshape(-1, 2, 512)
    kept = lax.dynamic_index_in_dim(total, core, 1, keepdims=False)
    sent = lax.dynamic_index_in_dim(total, 1 - core, 1, keepdims=False)
    residual = both(core, kept, swap(sent, "core", 1)).reshape(1, 32, 2, 256)

    row = group * 2 + core
    occ_energy = lax.dynamic_slice_in_dim(eps_occ, zl * 4 + lax.axis_index("y"), 1, 0)
    slab_energy = lax.dynamic_slice_in_dim(eps_vir, row * 2, 2, 0)
    denominator = (
        occ_energy[:, None, None, None]
        + eps_occ[None, :, None, None]
        - slab_energy[None, None, :, None]
        - eps_vir[None, None, None, :]
    )
    return residual / denominator


def solution(mesh):
    split = Mesh(mesh.devices.reshape(2, 4, 2, 8, 4), ("zh", "x", "core", "zl", "y"))
    row, inner = ("zh", "x", "core"), ("zl", "y")
    return jax.shard_map(
        step,
        mesh=split,
        in_specs=(
            P(row, None, inner, None),
            P(row, None, inner, None),
            P(None, row, None, inner),
            P(None, row, None, inner),
            P(),
            P(),
        ),
        out_specs=P(inner, None, row, None),
        check_vma=False,
    )
```

```python
import functools

import jax
import jax.numpy as jnp
from jax import lax
from jax.experimental import pallas as pl
from jax.experimental.pallas import tpu as pltpu
from jax.sharding import Mesh, PartitionSpec as P


VMEM = pl.BlockSpec(memory_space=pltpu.VMEM)
SMEM = pl.BlockSpec(memory_space=pltpu.SMEM)


def halves(value):
    high = value.astype(jnp.bfloat16)
    return high, (value - high.astype(jnp.float32)).astype(jnp.bfloat16)


def mul(a, b):
    return lax.dot_general(a, b, (((1,), (0,)), ((), ())), preferred_element_type=jnp.float32)


def every_eighth(lanes, first, count):
    return jnp.concatenate([lanes[n, pl.ds(first, count, stride=8), :] for n in range(2)], axis=1)


def swap(value, axis, bit):
    length = lax.axis_size(axis)
    return lax.ppermute(value, axis, [(i, i ^ bit) for i in range(length)])


def weights_kernel(w_ref, high_ref, low_ref, lanes):
    rows = high_ref.shape[1]
    lanes[0] = w_ref[:, :128]
    lanes[1] = w_ref[:, 128:]
    for c in range(8):
        block = every_eighth(lanes, c, rows)
        high, low = halves(block.T)
        high_ref[pl.ds(c * 256, 256), :] = high
        low_ref[pl.ds(c * 256, 256), :] = low


def weights(integrals):
    flat = integrals.reshape(-1, 256)
    rows = flat.shape[0] // 8
    step = 128
    return pl.pallas_call(
        weights_kernel,
        grid=(rows // step,),
        in_specs=[pl.BlockSpec((step * 8, 256), lambda n: (n, 0))],
        out_specs=[pl.BlockSpec((2048, step), lambda n: (0, n))] * 2,
        out_shape=[jax.ShapeDtypeStruct((2048, rows), jnp.bfloat16)] * 2,
        scratch_shapes=[pltpu.VMEM((2, step * 8, 128), jnp.float32)],
        cost_estimate=pl.CostEstimate(flops=0, bytes_accessed=32 << 20, transcendentals=0),
    )(flat)


def cross_kernel(place, own_ref, other_ref, *refs):
    t, out_ref, rows_ref = refs[:8], refs[8], refs[9]
    core, position, group = place[0], place[1], place[4]
    span = t[0].shape[0] // 4
    cross = jnp.zeros((span, 128), jnp.float32)
    for which, ref in ((core, own_ref), (1 - core, other_ref)):
        for k in range(16):
            for near in range(4):
                for far in range(8):
                    bits = ((far >> 2) & 1) | (far & 2) | ((far & 1) << 2)
                    target = (bits * 4 + near) ^ position
                    rows_ref[k % 2, pl.ds(pl.multiple_of(target * 8, 8), 8), :] = ref[near, far, k]
            wh, wl = halves(rows_ref[k % 2])
            first = pl.multiple_of((which * 2 + k % 2) * span, 8)
            high, low = halves(t[k // 2][pl.ds(first, span), :])
            cross += mul(high, wh) + mul(low, wh) + mul(high, wl)
    turned = cross.T
    for a in range(4):
        for q in range(8):
            for s in range(4):
                row = a * 32 + q * 4 + s
                out_ref[(q ^ group) * 4 + s, pl.ds(a, 1), :] = turned[row : row + 1]


def cross_term(place, own, other, pieces):
    span = pieces[0].shape[0] // 4
    return pl.pallas_call(
        cross_kernel,
        in_specs=[SMEM] + [VMEM] * 10,
        out_specs=VMEM,
        out_shape=jax.ShapeDtypeStruct((32, 4, span), jnp.float32),
        scratch_shapes=[pltpu.VMEM((2, 256, 128), jnp.float32)],
        cost_estimate=pl.CostEstimate(flops=3 << 30, bytes_accessed=8 << 20, transcendentals=0),
    )(place, own, other, *pieces)


def terms_kernel(place, *refs, late):
    t, refs = refs[:4], refs[4:]
    w_high, w_low, v_high, v_low, x_ref = refs[:5]
    if late:
        start, outs, (acc, lanes) = refs[5], refs[6:10], refs[10:]
    else:
        acc, lanes = refs[5:]
    core, near, target = place[0], place[2], place[3]
    span = t[0].shape[0] // 4
    js = span // 8
    first = 16 * js if late else 0
    if late:
        acc[...] = start[...]
    else:
        acc[:, pl.ds(16 * js, 16 * js), :] = jnp.zeros((8, 16 * js, 128), jnp.float32)
    for n, ref in enumerate(t):
        for half in range(2):
            lanes[half, pl.ds(n * 4 * span, 4 * span), :] = ref[:, half * 128 : half * 128 + 128]

    for c in range(8):
        high, low = halves(every_eighth(lanes, c, 16 * js))
        for which, wh, wl in ((core, w_high, w_low), (1 - core, v_high, v_low)):
            part = (
                mul(high, wh[pl.ds(c * 256, 256), :])
                + mul(low, wh[pl.ds(c * 256, 256), :])
                + mul(high, wl[pl.ds(c * 256, 256), :])
            )
            for n in range(4):
                piece = part[:, n * 128 : n * 128 + 128]
                if c == 0 and not late:
                    acc[which * 4 + n, pl.ds(first, 16 * js), :] = piece
                else:
                    acc[which * 4 + n, pl.ds(first, 16 * js), :] += piece

    x_high, x_low = halves(x_ref[:, 128:] if late else x_ref[:, :128])
    for j in range(js):
        rows = jnp.concatenate(
            [ref[pl.ds((s * js + j) * 8, 8), :] for ref in t for s in range(4)], axis=0
        )
        high, low = halves(rows)
        part = mul(x_high, high) + mul(x_low, high) + mul(x_high, low)
        for n in range(8):
            where = (n, pl.ds(j, 32, stride=js), slice(None))
            a, half = n // 2, n % 2
            acc[where] += part[a * 32 : a * 32 + 32, half * 128 : half * 128 + 128]

    if late:
        for d in range(4):
            for v in range(8):
                bits = ((v >> 2) & 1) | (v & 2) | ((v & 1) << 2)
                row = ((bits ^ target) * 4 + (near ^ d)) * js
                for n in range(8):
                    outs[d][v, :, n * 128 : n * 128 + 128] = acc[
                        n, pl.ds(pl.multiple_of(row, 8), js), :
                    ]


def terms(place, pieces, w, v, x, start=None):
    late = start is not None
    js = pieces[0].shape[0] // 32
    rows = 32 * js
    whole = jax.ShapeDtypeStruct((8, rows, 128), jnp.float32)
    args = (*pieces, *w, *v, x) + ((start,) if late else ())
    lanes = pltpu.VMEM((2, rows * 4, 128), jnp.float32)
    return pl.pallas_call(
        functools.partial(terms_kernel, late=late),
        in_specs=[SMEM] + [VMEM] * len(args),
        out_specs=[VMEM] * 4 if late else VMEM,
        out_shape=[jax.ShapeDtypeStruct((8, js, 1024), jnp.float32)] * 4 if late else whole,
        scratch_shapes=[pltpu.VMEM(whole.shape, jnp.float32), lanes] if late else [lanes],
        cost_estimate=pl.CostEstimate(
            flops=3 * rows * 1024 * 2048, bytes_accessed=20 << 20, transcendentals=0
        ),
    )(place, *args)


def both(core, own, other, dim=0):
    return jnp.where(
        core == 0, jnp.concatenate([own, other], dim), jnp.concatenate([other, own], dim)
    )


def turn(value, dim, flips):
    return jnp.take(value, jnp.arange(8) ^ flips, axis=dim, unique_indices=True, mode="clip")


def step(amplitudes, ladder_ints, cycle_direct, cycle_cross, eps_occ, eps_vir):
    zh, x, core = lax.axis_index("zh"), lax.axis_index("x"), lax.axis_index("core")
    zl, y = lax.axis_index("zl"), lax.axis_index("y")
    group = zh * 4 + x
    place = jnp.stack([core, zl * 4 + y, y, zl ^ group, group]).astype(jnp.int32)

    parts = amplitudes.reshape(2, 2, -1, 8, 256)
    mine = lax.dynamic_index_in_dim(parts, core, 1, keepdims=False)
    theirs = lax.dynamic_index_in_dim(parts, 1 - core, 1, keepdims=False)
    held = both(core, mine, swap(theirs, "core", 1))
    arrived = swap(held, "zh", 1)
    cycle_direct, cycle_cross, held = lax.optimization_barrier((cycle_direct, cycle_cross, held))
    pieces = [held] + [swap(held, "x", s) for s in (1, 2, 3)]

    def ordered(value):
        value = turn(turn(value.reshape(8, 4, 2, 8, 4, 8), 0, group), 3, group)
        return value.transpose(3, 4, 5, 2, 0, 1).reshape(32, 8, 64)

    local = jnp.stack([ordered(cycle_direct), ordered(cycle_cross)])
    paired = both(core, local, swap(local, "core", 1), 3)
    x_rows = paired[0].reshape(256, 128).T
    y_local = lax.dynamic_index_in_dim(
        paired[1].reshape(8, 2, 2, 8, 128), core, 1, keepdims=False
    ).reshape(16, 8, 128)
    for bit in (4, 2, 1):
        y_local = jnp.stack([y_local, swap(y_local, "zl", bit)])
    y_local = y_local.reshape(8, 16, 8, 128)
    ys = jnp.stack([y_local] + [swap(y_local, "y", s) for s in (1, 2, 3)])
    ys_other = swap(ys, "core", 1)

    swapped = swap(ladder_ints, "core", 1)
    w = weights(ladder_ints)
    v = weights(swapped)

    def flat(values):
        return [value.reshape(-1, 256) for value in values]

    start = terms(place, flat(pieces), w, v, x_rows)
    others = [arrived] + [swap(arrived, "x", s) for s in (1, 2, 3)]
    outs = terms(place, flat(others), w, v, x_rows, start)
    moved = {d: swap(outs[d], "y", d) for d in (2, 1, 3)}
    cross = cross_term(place, ys, ys_other, flat(pieces + others))
    cross = lax.all_to_all(cross, ("zl", "y"), 0, 0, tiled=True)
    cross = cross.reshape(32, 4, -1, 8).transpose(2, 1, 0, 3).reshape(-1, 2, 512)
    total = outs[0] + moved[1] + moved[3] + moved[2]
    for bit in (1, 2, 4):
        half = total.shape[0] // 2
        total = total[:half] + swap(total[half:], "zl", bit)
    total = total[0].reshape(-1, 2, 512) - cross
    kept = lax.dynamic_index_in_dim(total, core, 1, keepdims=False)
    sent = lax.dynamic_index_in_dim(total, 1 - core, 1, keepdims=False)
    residual = both(core, kept, swap(sent, "core", 1)).reshape(1, 32, 2, 256)

    row = group * 2 + core
    occ_energy = lax.dynamic_slice_in_dim(eps_occ, zl * 4 + lax.axis_index("y"), 1, 0)
    slab_energy = lax.dynamic_slice_in_dim(eps_vir, row * 2, 2, 0)
    denominator = (
        occ_energy[:, None, None, None]
        + eps_occ[None, :, None, None]
        - slab_energy[None, None, :, None]
        - eps_vir[None, None, None, :]
    )
    return residual / denominator


def solution(mesh):
    split = Mesh(mesh.devices.reshape(2, 4, 2, 8, 4), ("zh", "x", "core", "zl", "y"))
    row, inner = ("zh", "x", "core"), ("zl", "y")
    return jax.shard_map(
        step,
        mesh=split,
        in_specs=(
            P(row, None, inner, None),
            P(row, None, inner, None),
            P(None, row, None, inner),
            P(None, row, None, inner),
            P(),
            P(),
        ),
        out_specs=P(inner, None, row, None),
        check_vma=False,
    )
```
